32 devices in a mesh: dp: 4 (over z), ctx: 2 (over x), tp: 4 (over y, core).
Axes of the slice: x: 2, y: 2, z: 4, core: 2. Of those that a mesh axis runs over, the one named last changes fastest.
Arguments:
- tokens: bfloat16 [512, 2048], P(('dp', 'ctx', 'tp')), may hold values from -6 to 6
- grad_out: bfloat16 [512, 2048], P(('dp', 'ctx', 'tp')), may hold values from -6 to 6
- expert_ids: int32 [512, 8], P(('dp', 'ctx')), may hold values from 0 to 63, all different within a row; in each aligned block of 64 rows (0 to 63, 64 to 127, ...) at most 16 rows name the same one
- router_weights: bfloat16 [512, 8], P(('dp', 'ctx')), may hold values from 0.029907227 to 0.3984375
- w_gate: bfloat16 [64, 2048, 1536], P(('dp', 'ctx'), None, 'tp'), may hold values from -0.125 to 0.125
- w_up: bfloat16 [64, 2048, 1536], P(('dp', 'ctx'), None, 'tp'), may hold values from -0.125 to 0.125
- w_down: bfloat16 [64, 1536, 2048], P(('dp', 'ctx'), 'tp'), may hold values from -0.15625 to 0.15625
Outputs:
- layer_out: bfloat16 [512, 2048], P(('dp', 'ctx', 'tp'))
- grad_tokens: bfloat16 [512, 2048], P(('dp', 'ctx', 'tp'))
- grad_w_gate: bfloat16 [64, 2048, 1536], P(('dp', 'ctx'), None, 'tp')
- grad_w_up: bfloat16 [64, 2048, 1536], P(('dp', 'ctx'), None, 'tp')
- grad_w_down: bfloat16 [64, 1536, 2048], P(('dp', 'ctx'), 'tp')
The draws below stay inside these ranges and needn't reach their ends.
Inputs may be any that keep to these rules, and one draw needn't show every extreme that they name: `expert_ids`: each row names 8 different experts. Among the tokens of one index of dp and ctx no expert is named by more than 16 of them, and in every draw some expert is named by exactly 16 of them.
All inputs are finite; a program needn't handle non-finite values.
Results may differ from the reference program's by a relative error of at most 0.012.
Values may be sent and summed in bfloat16 or wider, within the bound.
A program may use at most 384 MiB of HBM per device.

```python
import math
import jax
import jax.numpy as jnp
import numpy as np
from jax import lax

D = 2048
FF = 1536
EXPERTS = 64
TOPK = 8
TOK_DEV = 16
MOST = 16
TOKENS = 512
N_DP = 4
N_CTX = 2
N_TP = 4


def level_of(stream_key, shape, split, smallest, largest):
    factor_of, own = 1.0, jax.random.fold_in(stream_key, 6)
    for dim, blocks in split:
        heights = jnp.exp(jax.random.uniform(jax.random.fold_in(own, dim), (blocks,), jnp.float32, smallest / len(split), largest / len(split)))
        factor_of = factor_of * jnp.repeat(heights, shape[dim] // blocks).reshape([-1 if axis == dim else 1 for axis in range(len(shape))])
    return factor_of


def assign_block(own_key, own, number, rows, count, top, bound, slope):
    sequence = jax.random.permutation(own_key, count)
    packed, usual = load_shares(count, rows * top, bound, slope, True), load_shares(count, rows * top, bound, slope, False)
    places = jnp.arange(count)

    def named(sizes, offset_by):
        used = int((sizes > 0).sum())
        fixed = max(1, used // 4)
        moved = fixed + (places - fixed + offset_by * (used - fixed)) % max(1, count - fixed)
        return jnp.zeros((count,), jnp.int32).at[sequence[jnp.where(places < fixed, places, moved)]].set(jnp.asarray(sizes, jnp.int32))

    sizes = jnp.where(number % 4 == 0, named(packed, number // 4), named(usual, number - number // 4 - 1))
    mixed = jax.random.permutation(jax.random.fold_in(own, 3), count)
    donor, taker = mixed[0:count // 2 * 2:2], mixed[1:count // 2 * 2:2]
    slack = jnp.minimum(sizes[donor] - 1, bound - sizes[taker]) // 2
    slack = jnp.where((donor == sequence[0]) | (taker == sequence[0]) | (sizes[taker] == 0), 0, jnp.maximum(slack, 0))
    moved = jax.random.randint(jax.random.fold_in(own, 4), (count // 2,), 0, 1 << 20) % (slack + 1)
    sizes = sizes.at[donor].add(-moved).at[taker].add(moved)
    members = jnp.searchsorted(jnp.cumsum(sizes), jnp.arange(rows * top), side="right").astype(jnp.int32)
    table = members.reshape(top, rows).T
    table = table[jax.random.permutation(jax.random.fold_in(own, 1), rows)]
    offset_by = jax.random.randint(jax.random.fold_in(own, 2), (rows, 1), 0, top)
    return jnp.take_along_axis(table, (jnp.arange(top)[None, :] + offset_by) % top, axis=1)


def load_shares(count, total, most, slope, full):
    weights = [(1 << 20) // math.isqrt(rank ** slope) + 1 for rank in range(1, count + 1)]
    largest = most if full else min(most, max(-(-total // count), total * weights[0] // sum(weights)))
    least = 1 if total - largest >= count - 1 else 0
    counts, rest = [largest] + [least] * (count - 1), total - largest - least * (count - 1)
    while rest > 0:
        candidates = [i for i in range(1, count) if counts[i] < largest] or [i for i in range(1, count) if counts[i] < most]
        pool, remaining = sum([weights[i] for i in candidates]), rest
        for i in candidates:
            addition = min(most - counts[i], max(1, remaining * weights[i] // pool), rest)
            counts[i] = counts[i] + addition
            rest = rest - addition
    return np.array(counts)


def normal_values(key, dims, width, reach, shards=(), kind=jnp.bfloat16):
    values = width * jax.random.normal(key, dims, jnp.float32)
    if shards:
        values = values * level_of(key, dims, shards, -0.22, 0.18)
    return jnp.clip(values, -reach, reach).astype(kind)


def setup_inputs(seed: int = 0) -> dict:
    key_of = jax.random.split(jax.random.key(seed), 8)
    tokens = normal_values(key_of[0], (TOKENS, D), 1.0, 6.0, ((0, 32),))
    grad_out = normal_values(key_of[1], (TOKENS, D), 1.0, 6.0, ((0, 32),))
    expert_ids_keys = jax.random.split(jax.random.fold_in(key_of[2], 1), TOKENS // (TOK_DEV * N_TP))
    expert_ids_turns = jax.random.permutation(jax.random.fold_in(key_of[2], 3), TOKENS // (TOK_DEV * N_TP))
    expert_ids = jax.vmap(lambda own, number: assign_block(jax.random.fold_in(key_of[2], 2), own, number, TOK_DEV * N_TP, EXPERTS, TOPK, MOST, 2))(expert_ids_keys, expert_ids_turns).reshape((TOKENS, TOPK))
    router_weights = jnp.clip(jnp.exp(math.log(0.3984375) - 2.5894505 * jax.random.uniform(key_of[3], (TOKENS, TOPK), jnp.float32) ** level_of(key_of[3], (TOKENS, TOPK), ((0, 8),), -0.2, 0.2)), 0.029907227, 0.3984375).astype(jnp.bfloat16)
    w_gate = normal_values(key_of[4], (EXPERTS, D, FF), D ** -0.5, 0.125, ((0, 8), (2, 4)))
    w_up = normal_values(key_of[5], (EXPERTS, D, FF), D ** -0.5, 0.125, ((0, 8), (2, 4)))
    w_down = normal_values(key_of[6], (EXPERTS, FF, D), FF ** -0.5, 0.15625, ((0, 8), (1, 4)))
    return dict(tokens=tokens, grad_out=grad_out, expert_ids=expert_ids, router_weights=router_weights, w_gate=w_gate, w_up=w_up, w_down=w_down)


def slot_ranks(group_ids):
    onehot = (group_ids[:, None] == jnp.arange(EXPERTS, dtype=jnp.int32)[None, :]).astype(jnp.int32)
    earlier = jnp.cumsum(onehot, axis=0) - onehot
    return jnp.sum(earlier * onehot, axis=1).astype(jnp.int32)


def round_trip(values):
    return lax.optimization_barrier(values.astype(jnp.bfloat16)).astype(jnp.float32)


def expert_pass(operands):
    inputs, cotangent, weights, gate_w, up_w, down_w = operands
    hidden_share = FF // N_TP
    gate = jnp.dot(inputs, gate_w, preferred_element_type=jnp.float32)
    upward = jnp.dot(inputs, up_w, preferred_element_type=jnp.float32)
    sigmoid_gate = jax.nn.sigmoid(gate)
    row_scale = weights.astype(jnp.float32)[:, None]
    activation = (row_scale * gate * sigmoid_gate * upward).astype(jnp.bfloat16)
    parts = jnp.einsum("rjf,jfd->rjd", activation.reshape(-1, N_TP, hidden_share).astype(jnp.float32),
                       down_w.reshape(N_TP, hidden_share, D).astype(jnp.float32))
    output_rows = jnp.sum(round_trip(parts), axis=1)
    backward = lax.dot_general(cotangent, down_w, (((1,), (1,)), ((), ())), preferred_element_type=jnp.float32)
    grad_gate_pre = (backward * row_scale * upward * sigmoid_gate * (1.0 + gate * (1.0 - sigmoid_gate))).astype(jnp.bfloat16)
    grad_up_pre = (backward * row_scale * gate * sigmoid_gate).astype(jnp.bfloat16)
    grad_down = lax.dot_general(activation, cotangent, (((0,), (0,)), ((), ())), preferred_element_type=jnp.float32).astype(jnp.bfloat16)
    grad_gate = lax.dot_general(inputs, grad_gate_pre, (((0,), (0,)), ((), ())), preferred_element_type=jnp.float32).astype(jnp.bfloat16)
    grad_up = lax.dot_general(inputs, grad_up_pre, (((0,), (0,)), ((), ())), preferred_element_type=jnp.float32).astype(jnp.bfloat16)
    input_parts = jnp.einsum("rjf,djf->rjd", grad_gate_pre.reshape(-1, N_TP, hidden_share).astype(jnp.float32),
                             gate_w.reshape(D, N_TP, hidden_share).astype(jnp.float32))
    input_parts = input_parts + jnp.einsum("rjf,djf->rjd", grad_up_pre.reshape(-1, N_TP, hidden_share).astype(jnp.float32),
                                           up_w.reshape(D, N_TP, hidden_share).astype(jnp.float32))
    input_rows = jnp.sum(round_trip(input_parts), axis=1)
    return output_rows, input_rows, grad_gate, grad_up, grad_down


def reference(tokens, grad_out, expert_ids, router_weights, w_gate, w_up, w_down):
    group_rows = TOK_DEV * N_TP
    group_count = N_DP * N_CTX
    expert_rows = group_count * MOST
    grouped = expert_ids.reshape(group_count, group_rows * TOPK)
    ranks = lax.map(slot_ranks, grouped)
    group_index = jnp.arange(group_count, dtype=jnp.int32)[:, None]
    slots = (grouped * expert_rows + group_index * MOST + ranks).astype(jnp.int32).reshape(TOKENS, TOPK)
    assignments = TOKENS * TOPK
    source = jnp.full((EXPERTS * expert_rows,), assignments, jnp.int32).at[slots.reshape(-1)].set(
        jnp.arange(assignments, dtype=jnp.int32))
    token_of = source // TOPK
    padded_tokens = jnp.concatenate([tokens, jnp.zeros((1, D), jnp.bfloat16)], axis=0)
    padded_grads = jnp.concatenate([grad_out, jnp.zeros((1, D), jnp.bfloat16)], axis=0)
    padded_weights = jnp.concatenate([router_weights.reshape(-1), jnp.zeros((1,), jnp.bfloat16)], axis=0)
    inputs = padded_tokens[token_of].reshape(EXPERTS, expert_rows, D)
    cotangents = padded_grads[token_of].reshape(EXPERTS, expert_rows, D)
    scales = padded_weights[source].reshape(EXPERTS, expert_rows)
    results = lax.map(expert_pass, (inputs, cotangents, scales, w_gate, w_up, w_down))
    output_table = results[0].reshape(EXPERTS * expert_rows, D)
    input_table = results[1].reshape(EXPERTS * expert_rows, D)

    def combine(table):
        def add_pick(running, column):
            return running + table[column], None
        summed, unused = lax.scan(add_pick, jnp.zeros((TOKENS, D), jnp.float32), slots.T)
        return summed.astype(jnp.bfloat16)

    return combine(output_table), combine(input_table), results[2], results[3], results[4]
```

```python
import jax
import jax.numpy as jnp
from jax import lax
from jax.experimental import pallas as pl
from jax.experimental.pallas import tpu as pltpu
from jax.sharding import PartitionSpec as P

contract_last = (((1,), (1,)), ((), ()))
contract_first = (((0,), (0,)), ((), ()))


def swiglu_rows(inputs, cotangent, row_weights, gate_w, up_w, down_w):
    gate = jnp.dot(inputs, gate_w, preferred_element_type=jnp.float32)
    upward = jnp.dot(inputs, up_w, preferred_element_type=jnp.float32)
    sigmoid_gate = jax.nn.sigmoid(gate)
    row_scale = row_weights.astype(jnp.float32)[:, None]
    activation = (row_scale * gate * sigmoid_gate * upward).astype(jnp.bfloat16)
    output_rows = jnp.dot(activation, down_w, preferred_element_type=jnp.float32).astype(
        jnp.bfloat16
    )
    backward = lax.dot_general(cotangent, down_w, contract_last, preferred_element_type=jnp.float32)
    grad_gate_pre = (
        backward * row_scale * upward * sigmoid_gate * (1.0 + gate * (1.0 - sigmoid_gate))
    ).astype(jnp.bfloat16)
    grad_up_pre = (backward * row_scale * gate * sigmoid_gate).astype(jnp.bfloat16)
    input_rows = (
        lax.dot_general(grad_gate_pre, gate_w, contract_last, preferred_element_type=jnp.float32)
        + lax.dot_general(grad_up_pre, up_w, contract_last, preferred_element_type=jnp.float32)
    ).astype(jnp.bfloat16)
    grad_down = lax.dot_general(
        activation, cotangent, contract_first, preferred_element_type=jnp.float32
    )
    grad_gate = lax.dot_general(
        inputs, grad_gate_pre, contract_first, preferred_element_type=jnp.float32
    )
    grad_up = lax.dot_general(
        inputs, grad_up_pre, contract_first, preferred_element_type=jnp.float32
    )
    return (output_rows, input_rows, grad_gate, grad_up, grad_down)


def shards(tokens, grad_out, expert_ids, router_weights, w_gate, w_up, w_down):
    expert_devices = lax.axis_size(("dp", "ctx"))
    group_rows, top_count = expert_ids.shape
    local_experts = w_gate.shape[0]
    expert_total = expert_devices * local_experts
    slot_most = 2 * group_rows * top_count // expert_total
    model_width = tokens.shape[1]
    group_tokens, group_grads = (
        lax.all_to_all(tokens, "tp", split_axis=1, concat_axis=0, tiled=True),
        lax.all_to_all(grad_out, "tp", split_axis=1, concat_axis=0, tiled=True),
    )
    carried = group_tokens.shape[1]
    flat_ids = expert_ids.reshape(-1)
    onehot = (flat_ids[:, None] == jnp.arange(expert_total, dtype=jnp.int32)[None, :]).astype(
        jnp.int32
    )
    earlier = jnp.cumsum(onehot, axis=0) - onehot
    ranks = jnp.sum(earlier * onehot, axis=1)
    slots = flat_ids * slot_most + ranks
    assignments = group_rows * top_count
    source = (
        jnp.full((expert_total * slot_most,), assignments, jnp.int32)
        .at[slots]
        .set(jnp.arange(assignments, dtype=jnp.int32))
    )
    token_of = source // top_count
    zero_row = jnp.zeros((1, carried), jnp.bfloat16)
    send_tokens = jnp.concatenate([group_tokens, zero_row], axis=0)[token_of].reshape(
        expert_devices, local_experts * slot_most, carried
    )
    send_grads = jnp.concatenate([group_grads, zero_row], axis=0)[token_of].reshape(
        expert_devices, local_experts * slot_most, carried
    )
    send_weights = jnp.concatenate(
        [router_weights.reshape(-1), jnp.zeros((1,), jnp.bfloat16)], axis=0
    )[source].reshape(expert_devices, local_experts * slot_most)
    recv_tokens, recv_grads, recv_weights = (
        lax.all_to_all(send_tokens, ("dp", "ctx"), split_axis=0, concat_axis=0, tiled=True),
        lax.all_to_all(send_grads, ("dp", "ctx"), split_axis=0, concat_axis=0, tiled=True),
        lax.all_to_all(send_weights, ("dp", "ctx"), split_axis=0, concat_axis=0, tiled=True),
    )
    recv_tokens, recv_grads = (
        lax.all_gather(recv_tokens, "tp", axis=2, tiled=True),
        lax.all_gather(recv_grads, "tp", axis=2, tiled=True),
    )
    token_grid = recv_tokens.reshape(expert_devices, local_experts, slot_most, model_width)
    grad_grid = recv_grads.reshape(expert_devices, local_experts, slot_most, model_width)
    weight_grid = recv_weights.reshape(expert_devices, local_experts, slot_most)
    outputs = []
    for expert_index in range(local_experts):
        outputs.append(
            swiglu_rows(
                token_grid[:, expert_index].reshape(-1, model_width),
                grad_grid[:, expert_index].reshape(-1, model_width),
                weight_grid[:, expert_index].reshape(-1),
                w_gate[expert_index],
                w_up[expert_index],
                w_down[expert_index],
            )
        )
    out_rows = jnp.stack(
        [entry[0].reshape(expert_devices, slot_most, model_width) for entry in outputs], axis=1
    ).reshape(expert_devices, local_experts * slot_most, model_width)
    in_rows = jnp.stack(
        [entry[1].reshape(expert_devices, slot_most, model_width) for entry in outputs], axis=1
    ).reshape(expert_devices, local_experts * slot_most, model_width)
    grad_gate = jnp.stack([entry[2] for entry in outputs], axis=0).astype(jnp.bfloat16)
    grad_up = jnp.stack([entry[3] for entry in outputs], axis=0).astype(jnp.bfloat16)
    grad_down = jnp.stack([entry[4] for entry in outputs], axis=0).astype(jnp.bfloat16)
    slot_grid = slots.reshape(group_rows, top_count)

    def combine(table):
        picked = table.reshape(expert_total * slot_most, -1)[slot_grid]
        return jnp.sum(picked, axis=1)

    column_out, column_in = (
        lax.psum_scatter(
            out_rows.astype(jnp.float32).astype(jnp.bfloat16), "tp", scatter_dimension=2, tiled=True
        ).astype(jnp.float32),
        lax.psum_scatter(
            in_rows.astype(jnp.float32).astype(jnp.bfloat16), "tp", scatter_dimension=2, tiled=True
        ).astype(jnp.float32),
    )
    back_out, back_in = (
        lax.all_to_all(
            column_out.astype(jnp.bfloat16), ("dp", "ctx"), split_axis=0, concat_axis=0, tiled=True
        ).astype(column_out.dtype),
        lax.all_to_all(
            column_in.astype(jnp.bfloat16), ("dp", "ctx"), split_axis=0, concat_axis=0, tiled=True
        ).astype(column_in.dtype),
    )
    layer_out, grad_tokens = (
        lax.all_to_all(
            combine(back_out).astype(jnp.bfloat16), "tp", split_axis=0, concat_axis=1, tiled=True
        ).astype(jnp.float32),
        lax.all_to_all(
            combine(back_in).astype(jnp.bfloat16), "tp", split_axis=0, concat_axis=1, tiled=True
        ).astype(jnp.float32),
    )
    return (
        layer_out.astype(jnp.bfloat16),
        grad_tokens.astype(jnp.bfloat16),
        grad_gate,
        grad_up,
        grad_down,
    )


def select_rows(order, row_count):
    rows = lax.broadcasted_iota(jnp.int32, (row_count, order.shape[-1]), 0)
    return rows == order


def rows_kernel(
    tokens, grads, order_row, scale_row, order_col, gate_w, up_w, down_w,
    inputs_out, cotangent_out, act_out, gate_pre_out, up_pre_out, sums_out,
    out_rows, in_rows,
):
    f32, bf16 = jnp.float32, jnp.bfloat16
    expert = pl.program_id(0)
    expert_count = order_col.shape[1]
    row_count = inputs_out.shape[1]
    token_count, width = tokens.shape
    picked = select_rows(order_row[0], row_count)
    row_scale = jnp.sum(jnp.where(picked, scale_row[0], 0.0), axis=1, keepdims=True)
    pick = jnp.where(picked, 1.0, 0.0).astype(bf16)
    inputs = jnp.dot(pick, tokens[...], preferred_element_type=f32).astype(bf16)
    cotangent = jnp.dot(pick, grads[...], preferred_element_type=f32).astype(bf16)
    inputs_out[0] = inputs
    cotangent_out[0] = cotangent
    gate = jnp.dot(inputs, gate_w[0], preferred_element_type=f32)
    upward = jnp.dot(inputs, up_w[0], preferred_element_type=f32)
    backward = lax.dot_general(cotangent, down_w[0], contract_last, preferred_element_type=f32)
    sigmoid_gate = jax.nn.sigmoid(gate)
    silu = row_scale * gate * sigmoid_gate
    act = (silu * upward).astype(bf16)
    gate_pre = (
        backward * row_scale * upward * sigmoid_gate * (1.0 + gate * (1.0 - sigmoid_gate))
    ).astype(bf16)
    up_pre = (backward * silu).astype(bf16)
    act_out[0] = act
    gate_pre_out[0] = gate_pre
    up_pre_out[0] = up_pre
    here = pl.ds(pl.multiple_of(expert * row_count, row_count), row_count)
    out_rows[here, :] = jnp.dot(act, down_w[0], preferred_element_type=f32).astype(bf16)
    in_rows[here, :] = (
        lax.dot_general(gate_pre, gate_w[0], contract_last, preferred_element_type=f32)
        + lax.dot_general(up_pre, up_w[0], contract_last, preferred_element_type=f32)
    ).astype(bf16)

    @pl.when(expert == expert_count - 1)
    def _():
        lanes = lax.broadcasted_iota(jnp.int32, (token_count, row_count), 1)
        place = jnp.concatenate(
            [
                jnp.where(lanes == order_col[:, e : e + 1], 1.0, 0.0).astype(bf16)
                for e in range(expert_count)
            ],
            axis=1,
        )
        sums_out[:, :width] = jnp.dot(
            place, out_rows[...], preferred_element_type=f32
        ).astype(bf16)
        sums_out[:, width:] = jnp.dot(
            place, in_rows[...], preferred_element_type=f32
        ).astype(bf16)


def weights_kernel(inputs, cotangent, act, gate_pre, up_pre, gate_out, up_out, down_out):
    f32, bf16 = jnp.float32, jnp.bfloat16
    gate_out[0] = lax.dot_general(
        inputs[0], gate_pre[0], contract_first, preferred_element_type=f32
    ).astype(bf16)
    up_out[0] = lax.dot_general(
        inputs[0], up_pre[0], contract_first, preferred_element_type=f32
    ).astype(bf16)
    down_out[0] = lax.dot_general(
        act[0], cotangent[0], contract_first, preferred_element_type=f32
    ).astype(bf16)


def gathered_shards(tokens, grad_out, expert_ids, router_weights, w_gate, w_up, w_down):
    f32, bf16, i32 = jnp.float32, jnp.bfloat16, jnp.int32
    axes = ("dp", "ctx", "tp")
    own_tokens, width = tokens.shape
    group_rows, top_count = expert_ids.shape
    experts, _, hidden = w_gate.shape
    groups = lax.axis_size(("dp", "ctx"))
    row_count = groups * (2 * group_rows * top_count // (groups * experts))
    start = lax.axis_index("tp") * own_tokens
    own_ids = lax.dynamic_slice_in_dim(expert_ids, start, own_tokens, 0)
    own_weights = lax.dynamic_slice_in_dim(router_weights, start, own_tokens, 0)
    routing = jnp.concatenate(
        [own_ids.astype(bf16), own_weights, jnp.zeros((own_tokens, 128 - 2 * top_count), bf16)],
        axis=1,
    )
    carried = lax.all_gather(
        jnp.concatenate([tokens, grad_out, routing], axis=1), axes, axis=0, tiled=True
    )
    total = carried.shape[0]
    ids = carried[:, 2 * width : 2 * width + top_count].astype(i32)
    weights = carried[:, 2 * width + top_count : 2 * width + 2 * top_count].astype(f32)
    first = lax.axis_index(("dp", "ctx")) * experts
    named = ids[:, None, :] == (first + jnp.arange(experts, dtype=i32))[None, :, None]
    scale = jnp.sum(jnp.where(named, weights[:, None, :], 0.0), axis=2)
    hit = jnp.any(named, axis=2)
    place = jnp.arange(total, dtype=i32)
    earlier = (place[:, None] > place[None, :]).astype(bf16)
    rank = jnp.dot(earlier, hit.astype(bf16), preferred_element_type=f32).astype(i32)
    order_col = jnp.where(hit, rank, -1)
    order_row = order_col.T.reshape(experts, 1, total)
    scale_row = scale.T.reshape(experts, 1, total)

    whole = lambda shape, column=0: pl.BlockSpec(shape, lambda e: (0, column))
    each = lambda *shape: pl.BlockSpec((1, *shape), lambda e: (e, 0, 0))
    rows_shape = lambda n: jax.ShapeDtypeStruct((experts, row_count, n), bf16)
    matmul = 2 * experts * row_count * width * hidden
    inputs, cotangent, act, gate_pre, up_pre, sums = pl.pallas_call(
        rows_kernel,
        grid=(experts,),
        in_specs=[
            whole((total, width)),
            whole((total, width), 1),
            each(1, total),
            each(1, total),
            whole((total, experts)),
            each(width, hidden),
            each(width, hidden),
            each(hidden, width),
        ],
        out_specs=[
            each(row_count, width),
            each(row_count, width),
            each(row_count, hidden),
            each(row_count, hidden),
            each(row_count, hidden),
            whole((total, 2 * width)),
        ],
        out_shape=[
            rows_shape(width),
            rows_shape(width),
            rows_shape(hidden),
            rows_shape(hidden),
            rows_shape(hidden),
            jax.ShapeDtypeStruct((total, 2 * width), bf16),
        ],
        scratch_shapes=[
            pltpu.VMEM((experts * row_count, width), bf16),
            pltpu.VMEM((experts * row_count, width), bf16),
        ],
        compiler_params=pltpu.CompilerParams(vmem_limit_bytes=60 << 20),
        cost_estimate=pl.CostEstimate(
            flops=6 * matmul, bytes_accessed=6 * experts * width * hidden, transcendentals=0
        ),
        name="expert_rows",
    )(carried, carried, order_row, scale_row, order_col, w_gate, w_up, w_down)
    summed = lax.psum_scatter(sums, axes, scatter_dimension=0, tiled=True)
    grad_gate, grad_up, grad_down = pl.pallas_call(
        weights_kernel,
        grid=(experts,),
        in_specs=[
            each(row_count, width),
            each(row_count, width),
            each(row_count, hidden),
            each(row_count, hidden),
            each(row_count, hidden),
        ],
        out_specs=[each(width, hidden), each(width, hidden), each(hidden, width)],
        out_shape=[
            jax.ShapeDtypeStruct(w_gate.shape, bf16),
            jax.ShapeDtypeStruct(w_up.shape, bf16),
            jax.ShapeDtypeStruct(w_down.shape, bf16),
        ],
        compiler_params=pltpu.CompilerParams(vmem_limit_bytes=60 << 20),
        cost_estimate=pl.CostEstimate(
            flops=3 * matmul, bytes_accessed=6 * experts * width * hidden, transcendentals=0
        ),
        name="expert_weights",
    )(inputs, cotangent, act, gate_pre, up_pre)
    return summed[:, :width], summed[:, width:], grad_gate, grad_up, grad_down


def solution(mesh):
    def per_device(tokens, *rest):
        devices = lax.axis_size(("dp", "ctx", "tp"))
        few = tokens.shape[0] * devices <= 1024
        return (gathered_shards if few else shards)(tokens, *rest)

    placed = (
        P(("dp", "ctx", "tp"), None),
        P(("dp", "ctx", "tp"), None),
        P(("dp", "ctx"), None),
        P(("dp", "ctx"), None),
        P(("dp", "ctx"), None, "tp"),
        P(("dp", "ctx"), None, "tp"),
        P(("dp", "ctx"), "tp", None),
    )
    return jax.shard_map(
        per_device,
        mesh=mesh,
        in_specs=placed,
        out_specs=(
            P(("dp", "ctx", "tp"), None),
            P(("dp", "ctx", "tp"), None),
            P(("dp", "ctx"), None, "tp"),
            P(("dp", "ctx"), None, "tp"),
            P(("dp", "ctx"), "tp", None),
        ),
        check_vma=False,
    )
```

```python
import jax
import jax.numpy as jnp
from jax import lax
from jax.experimental import pallas as pl
from jax.experimental.pallas import tpu as pltpu
from jax.sharding import PartitionSpec as P

contract_last = (((1,), (1,)), ((), ()))
contract_first = (((0,), (0,)), ((), ()))


def swiglu_rows(inputs, cotangent, row_weights, gate_w, up_w, down_w):
    gate = jnp.dot(inputs, gate_w, preferred_element_type=jnp.float32)
    upward = jnp.dot(inputs, up_w, preferred_element_type=jnp.float32)
    sigmoid_gate = jax.nn.sigmoid(gate)
    row_scale = row_weights.astype(jnp.float32)[:, None]
    activation = (row_scale * gate * sigmoid_gate * upward).astype(jnp.bfloat16)
    output_rows = jnp.dot(activation, down_w, preferred_element_type=jnp.float32).astype(
        jnp.bfloat16
    )
    backward = lax.dot_general(cotangent, down_w, contract_last, preferred_element_type=jnp.float32)
    grad_gate_pre = (
        backward * row_scale * upward * sigmoid_gate * (1.0 + gate * (1.0 - sigmoid_gate))
    ).astype(jnp.bfloat16)
    grad_up_pre = (backward * row_scale * gate * sigmoid_gate).astype(jnp.bfloat16)
    input_rows = (
        lax.dot_general(grad_gate_pre, gate_w, contract_last, preferred_element_type=jnp.float32)
        + lax.dot_general(grad_up_pre, up_w, contract_last, preferred_element_type=jnp.float32)
    ).astype(jnp.bfloat16)
    grad_down = lax.dot_general(
        activation, cotangent, contract_first, preferred_element_type=jnp.float32
    )
    grad_gate = lax.dot_general(
        inputs, grad_gate_pre, contract_first, preferred_element_type=jnp.float32
    )
    grad_up = lax.dot_general(
        inputs, grad_up_pre, contract_first, preferred_element_type=jnp.float32
    )
    return (output_rows, input_rows, grad_gate, grad_up, grad_down)


def shards(tokens, grad_out, expert_ids, router_weights, w_gate, w_up, w_down):
    expert_devices = lax.axis_size(("dp", "ctx"))
    group_rows, top_count = expert_ids.shape
    local_experts = w_gate.shape[0]
    expert_total = expert_devices * local_experts
    slot_most = 2 * group_rows * top_count // expert_total
    model_width = tokens.shape[1]
    group_tokens, group_grads = (
        lax.all_to_all(tokens, "tp", split_axis=1, concat_axis=0, tiled=True),
        lax.all_to_all(grad_out, "tp", split_axis=1, concat_axis=0, tiled=True),
    )
    carried = group_tokens.shape[1]
    flat_ids = expert_ids.reshape(-1)
    onehot = (flat_ids[:, None] == jnp.arange(expert_total, dtype=jnp.int32)[None, :]).astype(
        jnp.int32
    )
    earlier = jnp.cumsum(onehot, axis=0) - onehot
    ranks = jnp.sum(earlier * onehot, axis=1)
    slots = flat_ids * slot_most + ranks
    assignments = group_rows * top_count
    source = (
        jnp.full((expert_total * slot_most,), assignments, jnp.int32)
        .at[slots]
        .set(jnp.arange(assignments, dtype=jnp.int32))
    )
    token_of = source // top_count
    zero_row = jnp.zeros((1, carried), jnp.bfloat16)
    send_tokens = jnp.concatenate([group_tokens, zero_row], axis=0)[token_of].reshape(
        expert_devices, local_experts * slot_most, carried
    )
    send_grads = jnp.concatenate([group_grads, zero_row], axis=0)[token_of].reshape(
        expert_devices, local_experts * slot_most, carried
    )
    send_weights = jnp.concatenate(
        [router_weights.reshape(-1), jnp.zeros((1,), jnp.bfloat16)], axis=0
    )[source].reshape(expert_devices, local_experts * slot_most)
    recv_tokens, recv_grads, recv_weights = (
        lax.all_to_all(send_tokens, ("dp", "ctx"), split_axis=0, concat_axis=0, tiled=True),
        lax.all_to_all(send_grads, ("dp", "ctx"), split_axis=0, concat_axis=0, tiled=True),
        lax.all_to_all(send_weights, ("dp", "ctx"), split_axis=0, concat_axis=0, tiled=True),
    )
    recv_tokens, recv_grads = (
        lax.all_gather(recv_tokens, "tp", axis=2, tiled=True),
        lax.all_gather(recv_grads, "tp", axis=2, tiled=True),
    )
    token_grid = recv_tokens.reshape(expert_devices, local_experts, slot_most, model_width)
    grad_grid = recv_grads.reshape(expert_devices, local_experts, slot_most, model_width)
    weight_grid = recv_weights.reshape(expert_devices, local_experts, slot_most)
    outputs = []
    for expert_index in range(local_experts):
        outputs.append(
            swiglu_rows(
                token_grid[:, expert_index].reshape(-1, model_width),
                grad_grid[:, expert_index].reshape(-1, model_width),
                weight_grid[:, expert_index].reshape(-1),
                w_gate[expert_index],
                w_up[expert_index],
                w_down[expert_index],
            )
        )
    out_rows = jnp.stack(
        [entry[0].reshape(expert_devices, slot_most, model_width) for entry in outputs], axis=1
    ).reshape(expert_devices, local_experts * slot_most, model_width)
    in_rows = jnp.stack(
        [entry[1].reshape(expert_devices, slot_most, model_width) for entry in outputs], axis=1
    ).reshape(expert_devices, local_experts * slot_most, model_width)
    grad_gate = jnp.stack([entry[2] for entry in outputs], axis=0).astype(jnp.bfloat16)
    grad_up = jnp.stack([entry[3] for entry in outputs], axis=0).astype(jnp.bfloat16)
    grad_down = jnp.stack([entry[4] for entry in outputs], axis=0).astype(jnp.bfloat16)
    slot_grid = slots.reshape(group_rows, top_count)

    def combine(table):
        picked = table.reshape(expert_total * slot_most, -1)[slot_grid]
        return jnp.sum(picked, axis=1)

    column_out, column_in = (
        lax.psum_scatter(
            out_rows.astype(jnp.float32).astype(jnp.bfloat16), "tp", scatter_dimension=2, tiled=True
        ).astype(jnp.float32),
        lax.psum_scatter(
            in_rows.astype(jnp.float32).astype(jnp.bfloat16), "tp", scatter_dimension=2, tiled=True
        ).astype(jnp.float32),
    )
    back_out, back_in = (
        lax.all_to_all(
            column_out.astype(jnp.bfloat16), ("dp", "ctx"), split_axis=0, concat_axis=0, tiled=True
        ).astype(column_out.dtype),
        lax.all_to_all(
            column_in.astype(jnp.bfloat16), ("dp", "ctx"), split_axis=0, concat_axis=0, tiled=True
        ).astype(column_in.dtype),
    )
    layer_out, grad_tokens = (
        lax.all_to_all(
            combine(back_out).astype(jnp.bfloat16), "tp", split_axis=0, concat_axis=1, tiled=True
        ).astype(jnp.float32),
        lax.all_to_all(
            combine(back_in).astype(jnp.bfloat16), "tp", split_axis=0, concat_axis=1, tiled=True
        ).astype(jnp.float32),
    )
    return (
        layer_out.astype(jnp.bfloat16),
        grad_tokens.astype(jnp.bfloat16),
        grad_gate,
        grad_up,
        grad_down,
    )


def select_rows(order, row_count):
    rows = lax.broadcasted_iota(jnp.int32, (row_count, order.shape[-1]), 0)
    return rows == order


class Place:
    def __init__(self):
        self.ring = lax.axis_size("dp")
        self.z, self.x = lax.axis_index("dp"), lax.axis_index("ctx")
        tp = lax.axis_index("tp")
        self.y, self.c = tp // 2, tp % 2

    def device(self, z=None, x=None, y=None, c=None):
        pick = lambda value, own: own if value is None else value
        tp = pick(y, self.y) * 2 + pick(c, self.c)
        return (pick(z, self.z), pick(x, self.x), tp)

    def meet(self):
        barrier = pltpu.get_barrier_semaphore()
        others = [self.core_peer(), self.x_peer(), self.y_peer()]
        others += [self.device(z=lax.rem(self.z + k, self.ring)) for k in range(1, self.ring)]
        for other in others:
            pl.semaphore_signal(
                barrier, inc=1, device_id=other, device_id_type=pl.DeviceIdType.MESH
            )
        pl.semaphore_wait(barrier, len(others))

    def core_peer(self):
        return self.device(c=1 - self.c)

    def x_peer(self):
        return self.device(x=1 - self.x)

    def y_peer(self):
        return self.device(y=1 - self.y)


def start_send(source, target, send_sem, recv_sem, device):
    copy = pltpu.make_async_remote_copy(
        src_ref=source,
        dst_ref=target,
        send_sem=send_sem,
        recv_sem=recv_sem,
        device_id=device,
        device_id_type=pl.DeviceIdType.MESH,
    )
    copy.start()
    return copy


def gather_kernel(own_a, own_b, all_a, all_b, send_sems, recv_sems, local_sems):
    at = Place()
    z, x, y, c, ring = at.z, at.x, at.y, at.c, at.ring
    own, full = (own_a, own_b), (all_a, all_b)
    stay = []
    for h in range(2):
        copy = pltpu.make_async_copy(own[h], full[h].at[z, x, y, c], local_sems.at[h])
        copy.start()
        stay.append(copy)
    at.meet()
    sems = lambda stage, h, k: (send_sems.at[stage, h, k], recv_sems.at[stage, h, k])
    first, second, third, along = {}, {}, {}, {}
    peers = ((at.x_peer(), at.y_peer()), (at.y_peer(), at.x_peer()))
    for h in range(2):
        here = full[h].at[z, x, y, c]
        first[h, 0] = start_send(own[h], here, *sems(1, h, 0), peers[h][0])
        for k in range(1, ring):
            away = at.device(z=lax.rem(z + k, ring))
            along[h, k] = start_send(own[h], here, *sems(0, h, k), away)
    for copy in stay:
        copy.wait()
    for k in range(ring):
        zz = lax.rem(z - k + ring, ring)
        for h in range(2):
            if k > 0:
                along[h, k].wait_recv()
                block = full[h].at[zz, x, y, c]
                first[h, k] = start_send(block, block, *sems(1, h, k), peers[h][0])
    for k in range(ring):
        zz = lax.rem(z - k + ring, ring)
        for h in range(2):
            first[h, k].wait_recv()
            block = full[h].at[zz, :, y, c] if h == 0 else full[h].at[zz, x, :, c]
            second[h, k] = start_send(block, block, *sems(2, h, k), peers[h][1])
    for k in range(ring):
        zz = lax.rem(z - k + ring, ring)
        for h in range(2):
            second[h, k].wait_recv()
            block = full[h].at[zz, :, :, c]
            third[h, k] = start_send(block, block, *sems(3, h, k), at.core_peer())
    for copy in third.values():
        copy.wait_recv()
    for copies in (along, first, second, third):
        for copy in copies.values():
            copy.wait_send()


def gather_all(own_a, own_b):
    ring = lax.axis_size("dp")
    full = lambda own: jax.ShapeDtypeStruct((ring, 2, 2, 2, *own.shape), own.dtype)
    anywhere = pl.BlockSpec(memory_space=pl.ANY)
    return pl.pallas_call(
        gather_kernel,
        in_specs=[anywhere, anywhere],
        out_specs=[anywhere, anywhere],
        out_shape=[full(own_a), full(own_b)],
        scratch_shapes=[
            pltpu.SemaphoreType.DMA((4, 2, ring)),
            pltpu.SemaphoreType.DMA((4, 2, ring)),
            pltpu.SemaphoreType.DMA((2,)),
        ],
        compiler_params=pltpu.CompilerParams(collective_id=0, has_side_effects=True),
        name="gather_all",
    )(own_a, own_b)


def reduce_kernel(sums, out_a, out_b, got1, sum1, got2, sum2, got3, sum3, got4, send_sems, recv_sems):
    at = Place()
    z, x, y, c, ring = at.z, at.x, at.y, at.c, at.ring
    f32, bf16 = jnp.float32, jnp.bfloat16
    at.meet()
    sems = lambda stage, h, k: (send_sems.at[stage, h, k], recv_sems.at[stage, h, k])
    peers = ((at.y_peer(), at.x_peer()), (at.x_peer(), at.y_peer()))
    copies = [{}, {}, {}, {}]
    pairs = [(k, h) for k in range(ring) for h in range(2)]
    aim = [lax.rem(z + 1 + k, ring) for k in range(ring)]
    for k, h in pairs:
        copies[0][h, k] = start_send(
            sums.at[h, aim[k], :, :, 1 - c], got1.at[h, k], *sems(0, h, k), at.core_peer()
        )
    for k, h in pairs:
        copies[0][h, k].wait_recv()
        sum1[h, k] = (sums[h, aim[k], :, :, c].astype(f32) + got1[h, k].astype(f32)).astype(bf16)
        part = sum1.at[h, k, :, 1 - y] if h == 0 else sum1.at[h, k, 1 - x]
        copies[1][h, k] = start_send(part, got2.at[h, k], *sems(1, h, k), peers[h][0])
    for k, h in pairs:
        copies[1][h, k].wait_recv()
        mine = sum1[h, k, :, y] if h == 0 else sum1[h, k, x]
        sum2[h, k] = (mine.astype(f32) + got2[h, k].astype(f32)).astype(bf16)
        part = sum2.at[h, k, 1 - x] if h == 0 else sum2.at[h, k, 1 - y]
        copies[2][h, k] = start_send(part, got3.at[h, k], *sems(2, h, k), peers[h][1])
    for k, h in pairs:
        copies[2][h, k].wait_recv()
        mine = sum2[h, k, x] if h == 0 else sum2[h, k, y]
        sum3[h, k] = (mine.astype(f32) + got3[h, k].astype(f32)).astype(bf16)
        if k < ring - 1:
            copies[3][h, k] = start_send(
                sum3.at[h, k], got4.at[h, k], *sems(3, h, k), at.device(z=aim[k])
            )
    for h, out in enumerate((out_a, out_b)):
        total = sum3[h, ring - 1].astype(f32)
        for k in range(ring - 1):
            copies[3][h, k].wait_recv()
            total = total + got4[h, k].astype(f32)
        out[...] = total.astype(bf16)
    for stage in copies:
        for copy in stage.values():
            copy.wait_send()


def reduce_all(sums):
    _, ring, _, _, _, rows, width = sums.shape
    out = jax.ShapeDtypeStruct((rows, width), sums.dtype)
    in_vmem = pl.BlockSpec(memory_space=pltpu.VMEM)
    table = lambda *lead: pltpu.VMEM((2, ring, *lead, rows, width), sums.dtype)
    return pl.pallas_call(
        reduce_kernel,
        in_specs=[in_vmem],
        out_specs=[in_vmem, in_vmem],
        out_shape=[out, out],
        scratch_shapes=[
            table(2, 2), table(2, 2), table(2), table(2), table(), table(), table(),
            pltpu.SemaphoreType.DMA((4, 2, ring)),
            pltpu.SemaphoreType.DMA((4, 2, ring)),
        ],
        compiler_params=pltpu.CompilerParams(
            collective_id=1, has_side_effects=True, vmem_limit_bytes=40 << 20
        ),
        name="reduce_all",
    )(sums)


def rows_kernel(
    tokens, grads, order_row, scale_row, order_col, gate_w, up_w, down_w,
    inputs_out, cotangent_out, act_out, gate_pre_out, up_pre_out, sums_out,
    out_rows, in_rows,
):
    f32, bf16 = jnp.float32, jnp.bfloat16
    expert = pl.program_id(0)
    expert_count = order_col.shape[1]
    row_count = inputs_out.shape[1]
    token_count, width = tokens.shape
    picked = select_rows(order_row[0], row_count)
    row_scale = jnp.sum(jnp.where(picked, scale_row[0], 0.0), axis=1, keepdims=True)
    pick = jnp.where(picked, 1.0, 0.0).astype(bf16)
    inputs = jnp.dot(pick, tokens[...], preferred_element_type=f32).astype(bf16)
    cotangent = jnp.dot(pick, grads[...], preferred_element_type=f32).astype(bf16)
    inputs_out[0] = inputs
    cotangent_out[0] = cotangent
    gate = jnp.dot(inputs, gate_w[0], preferred_element_type=f32)
    upward = jnp.dot(inputs, up_w[0], preferred_element_type=f32)
    backward = lax.dot_general(cotangent, down_w[0], contract_last, preferred_element_type=f32)
    sigmoid_gate = jax.nn.sigmoid(gate)
    silu = row_scale * gate * sigmoid_gate
    act = (silu * upward).astype(bf16)
    gate_pre = (
        backward * row_scale * upward * sigmoid_gate * (1.0 + gate * (1.0 - sigmoid_gate))
    ).astype(bf16)
    up_pre = (backward * silu).astype(bf16)
    act_out[0] = act
    gate_pre_out[0] = gate_pre
    up_pre_out[0] = up_pre
    here = pl.ds(pl.multiple_of(expert * row_count, row_count), row_count)
    out_rows[here, :] = jnp.dot(act, down_w[0], preferred_element_type=f32).astype(bf16)
    in_rows[here, :] = (
        lax.dot_general(gate_pre, gate_w[0], contract_last, preferred_element_type=f32)
        + lax.dot_general(up_pre, up_w[0], contract_last, preferred_element_type=f32)
    ).astype(bf16)

    @pl.when(expert == expert_count - 1)
    def _():
        lanes = lax.broadcasted_iota(jnp.int32, (token_count, row_count), 1)
        place = jnp.concatenate(
            [
                jnp.where(lanes == order_col[:, e : e + 1], 1.0, 0.0).astype(bf16)
                for e in range(expert_count)
            ],
            axis=1,
        )
        sums_out[0] = jnp.dot(
            place, out_rows[...], preferred_element_type=f32
        ).astype(bf16)
        sums_out[1] = jnp.dot(
            place, in_rows[...], preferred_element_type=f32
        ).astype(bf16)


def weights_kernel(inputs, cotangent, act, gate_pre, up_pre, gate_out, up_out, down_out):
    f32, bf16 = jnp.float32, jnp.bfloat16
    gate_out[0] = lax.dot_general(
        inputs[0], gate_pre[0], contract_first, preferred_element_type=f32
    ).astype(bf16)
    up_out[0] = lax.dot_general(
        inputs[0], up_pre[0], contract_first, preferred_element_type=f32
    ).astype(bf16)
    down_out[0] = lax.dot_general(
        act[0], cotangent[0], contract_first, preferred_element_type=f32
    ).astype(bf16)


def gathered_shards(tokens, grad_out, expert_ids, router_weights, w_gate, w_up, w_down):
    f32, bf16, i32 = jnp.float32, jnp.bfloat16, jnp.int32
    own_tokens, width = tokens.shape
    group_rows, top_count = expert_ids.shape
    experts, _, hidden = w_gate.shape
    groups = lax.axis_size(("dp", "ctx"))
    row_count = groups * (2 * group_rows * top_count // (groups * experts))
    start = lax.axis_index("tp") * own_tokens
    own_ids = lax.dynamic_slice_in_dim(expert_ids, start, own_tokens, 0)
    own_weights = lax.dynamic_slice_in_dim(router_weights, start, own_tokens, 0)
    routing = jnp.concatenate(
        [own_ids.astype(bf16), own_weights, jnp.zeros((own_tokens, 128 - 2 * top_count), bf16)],
        axis=1,
    )
    all_tokens, carried = gather_all(tokens, jnp.concatenate([grad_out, routing], axis=1))
    all_tokens, carried = all_tokens.reshape(-1, width), carried.reshape(-1, width + 128)
    total = carried.shape[0]
    ids = carried[:, width : width + top_count].astype(i32)
    weights = carried[:, width + top_count : width + 2 * top_count].astype(f32)
    first = lax.axis_index(("dp", "ctx")) * experts
    named = ids[:, None, :] == (first + jnp.arange(experts, dtype=i32))[None, :, None]
    scale = jnp.sum(jnp.where(named, weights[:, None, :], 0.0), axis=2)
    hit = jnp.any(named, axis=2)
    place = jnp.arange(total, dtype=i32)
    earlier = (place[:, None] > place[None, :]).astype(bf16)
    rank = jnp.dot(earlier, hit.astype(bf16), preferred_element_type=f32).astype(i32)
    order_col = jnp.where(hit, rank, -1)
    order_row = order_col.T.reshape(experts, 1, total)
    scale_row = scale.T.reshape(experts, 1, total)

    whole = lambda *shape: pl.BlockSpec(shape, lambda e: (0,) * len(shape))
    each = lambda *shape: pl.BlockSpec((1, *shape), lambda e: (e, 0, 0))
    rows_shape = lambda n: jax.ShapeDtypeStruct((experts, row_count, n), bf16)
    matmul = 2 * experts * row_count * width * hidden
    inputs, cotangent, act, gate_pre, up_pre, sums = pl.pallas_call(
        rows_kernel,
        grid=(experts,),
        in_specs=[
            whole(total, width),
            whole(total, width),
            each(1, total),
            each(1, total),
            whole(total, experts),
            each(width, hidden),
            each(width, hidden),
            each(hidden, width),
        ],
        out_specs=[
            each(row_count, width),
            each(row_count, width),
            each(row_count, hidden),
            each(row_count, hidden),
            each(row_count, hidden),
            whole(2, total, width),
        ],
        out_shape=[
            rows_shape(width),
            rows_shape(width),
            rows_shape(hidden),
            rows_shape(hidden),
            rows_shape(hidden),
            jax.ShapeDtypeStruct((2, total, width), bf16),
        ],
        scratch_shapes=[
            pltpu.VMEM((experts * row_count, width), bf16),
            pltpu.VMEM((experts * row_count, width), bf16),
        ],
        compiler_params=pltpu.CompilerParams(vmem_limit_bytes=60 << 20),
        cost_estimate=pl.CostEstimate(
            flops=6 * matmul, bytes_accessed=6 * experts * width * hidden, transcendentals=0
        ),
        name="expert_rows",
    )(all_tokens, carried, order_row, scale_row, order_col, w_gate, w_up, w_down)
    layer_out, grad_tokens = reduce_all(
        sums.reshape(2, lax.axis_size("dp"), 2, 2, 2, own_tokens, width)
    )
    grad_gate, grad_up, grad_down = pl.pallas_call(
        weights_kernel,
        grid=(experts,),
        in_specs=[
            each(row_count, width),
            each(row_count, width),
            each(row_count, hidden),
            each(row_count, hidden),
            each(row_count, hidden),
        ],
        out_specs=[each(width, hidden), each(width, hidden), each(hidden, width)],
        out_shape=[
            jax.ShapeDtypeStruct(w_gate.shape, bf16),
            jax.ShapeDtypeStruct(w_up.shape, bf16),
            jax.ShapeDtypeStruct(w_down.shape, bf16),
        ],
        compiler_params=pltpu.CompilerParams(vmem_limit_bytes=60 << 20),
        cost_estimate=pl.CostEstimate(
            flops=3 * matmul, bytes_accessed=6 * experts * width * hidden, transcendentals=0
        ),
        name="expert_weights",
    )(inputs, cotangent, act, gate_pre, up_pre)
    return layer_out, grad_tokens, grad_gate, grad_up, grad_down


def solution(mesh):
    def per_device(tokens, *rest):
        devices = lax.axis_size(("dp", "ctx", "tp"))
        few = tokens.shape[0] * devices <= 1024
        few = few and lax.axis_size("ctx") == 2 and lax.axis_size("tp") == 4
        return (gathered_shards if few else shards)(tokens, *rest)

    placed = (
        P(("dp", "ctx", "tp"), None),
        P(("dp", "ctx", "tp"), None),
        P(("dp", "ctx"), None),
        P(("dp", "ctx"), None),
        P(("dp", "ctx"), None, "tp"),
        P(("dp", "ctx"), None, "tp"),
        P(("dp", "ctx"), "tp", None),
    )
    return jax.shard_map(
        per_device,
        mesh=mesh,
        in_specs=placed,
        out_specs=(
            P(("dp", "ctx", "tp"), None),
            P(("dp", "ctx", "tp"), None),
            P(("dp", "ctx"), None, "tp"),
            P(("dp", "ctx"), None, "tp"),
            P(("dp", "ctx"), "tp", None),
        ),
        check_vma=False,
    )
```

```python
import jax
import jax.numpy as jnp
from jax import lax
from jax.experimental import pallas as pl
from jax.experimental.pallas import tpu as pltpu
from jax.sharding import PartitionSpec as P

contract_last = (((1,), (1,)), ((), ()))
contract_first = (((0,), (0,)), ((), ()))


def swiglu_rows(inputs, cotangent, row_weights, gate_w, up_w, down_w):
    gate = jnp.dot(inputs, gate_w, preferred_element_type=jnp.float32)
    upward = jnp.dot(inputs, up_w, preferred_element_type=jnp.float32)
    sigmoid_gate = jax.nn.sigmoid(gate)
    row_scale = row_weights.astype(jnp.float32)[:, None]
    activation = (row_scale * gate * sigmoid_gate * upward).astype(jnp.bfloat16)
    output_rows = jnp.dot(activation, down_w, preferred_element_type=jnp.float32).astype(
        jnp.bfloat16
    )
    backward = lax.dot_general(cotangent, down_w, contract_last, preferred_element_type=jnp.float32)
    grad_gate_pre = (
        backward * row_scale * upward * sigmoid_gate * (1.0 + gate * (1.0 - sigmoid_gate))
    ).astype(jnp.bfloat16)
    grad_up_pre = (backward * row_scale * gate * sigmoid_gate).astype(jnp.bfloat16)
    input_rows = (
        lax.dot_general(grad_gate_pre, gate_w, contract_last, preferred_element_type=jnp.float32)
        + lax.dot_general(grad_up_pre, up_w, contract_last, preferred_element_type=jnp.float32)
    ).astype(jnp.bfloat16)
    grad_down = lax.dot_general(
        activation, cotangent, contract_first, preferred_element_type=jnp.float32
    )
    grad_gate = lax.dot_general(
        inputs, grad_gate_pre, contract_first, preferred_element_type=jnp.float32
    )
    grad_up = lax.dot_general(
        inputs, grad_up_pre, contract_first, preferred_element_type=jnp.float32
    )
    return (output_rows, input_rows, grad_gate, grad_up, grad_down)


def shards(tokens, grad_out, expert_ids, router_weights, w_gate, w_up, w_down):
    expert_devices = lax.axis_size(("dp", "ctx"))
    group_rows, top_count = expert_ids.shape
    local_experts = w_gate.shape[0]
    expert_total = expert_devices * local_experts
    slot_most = 2 * group_rows * top_count // expert_total
    model_width = tokens.shape[1]
    group_tokens, group_grads = (
        lax.all_to_all(tokens, "tp", split_axis=1, concat_axis=0, tiled=True),
        lax.all_to_all(grad_out, "tp", split_axis=1, concat_axis=0, tiled=True),
    )
    carried = group_tokens.shape[1]
    flat_ids = expert_ids.reshape(-1)
    onehot = (flat_ids[:, None] == jnp.arange(expert_total, dtype=jnp.int32)[None, :]).astype(
        jnp.int32
    )
    earlier = jnp.cumsum(onehot, axis=0) - onehot
    ranks = jnp.sum(earlier * onehot, axis=1)
    slots = flat_ids * slot_most + ranks
    assignments = group_rows * top_count
    source = (
        jnp.full((expert_total * slot_most,), assignments, jnp.int32)
        .at[slots]
        .set(jnp.arange(assignments, dtype=jnp.int32))
    )
    token_of = source // top_count
    zero_row = jnp.zeros((1, carried), jnp.bfloat16)
    send_tokens = jnp.concatenate([group_tokens, zero_row], axis=0)[token_of].reshape(
        expert_devices, local_experts * slot_most, carried
    )
    send_grads = jnp.concatenate([group_grads, zero_row], axis=0)[token_of].reshape(
        expert_devices, local_experts * slot_most, carried
    )
    send_weights = jnp.concatenate(
        [router_weights.reshape(-1), jnp.zeros((1,), jnp.bfloat16)], axis=0
    )[source].reshape(expert_devices, local_experts * slot_most)
    recv_tokens, recv_grads, recv_weights = (
        lax.all_to_all(send_tokens, ("dp", "ctx"), split_axis=0, concat_axis=0, tiled=True),
        lax.all_to_all(send_grads, ("dp", "ctx"), split_axis=0, concat_axis=0, tiled=True),
        lax.all_to_all(send_weights, ("dp", "ctx"), split_axis=0, concat_axis=0, tiled=True),
    )
    recv_tokens, recv_grads = (
        lax.all_gather(recv_tokens, "tp", axis=2, tiled=True),
        lax.all_gather(recv_grads, "tp", axis=2, tiled=True),
    )
    token_grid = recv_tokens.reshape(expert_devices, local_experts, slot_most, model_width)
    grad_grid = recv_grads.reshape(expert_devices, local_experts, slot_most, model_width)
    weight_grid = recv_weights.reshape(expert_devices, local_experts, slot_most)
    outputs = []
    for expert_index in range(local_experts):
        outputs.append(
            swiglu_rows(
                token_grid[:, expert_index].reshape(-1, model_width),
                grad_grid[:, expert_index].reshape(-1, model_width),
                weight_grid[:, expert_index].reshape(-1),
                w_gate[expert_index],
                w_up[expert_index],
                w_down[expert_index],
            )
        )
    out_rows = jnp.stack(
        [entry[0].reshape(expert_devices, slot_most, model_width) for entry in outputs], axis=1
    ).reshape(expert_devices, local_experts * slot_most, model_width)
    in_rows = jnp.stack(
        [entry[1].reshape(expert_devices, slot_most, model_width) for entry in outputs], axis=1
    ).reshape(expert_devices, local_experts * slot_most, model_width)
    grad_gate = jnp.stack([entry[2] for entry in outputs], axis=0).astype(jnp.bfloat16)
    grad_up = jnp.stack([entry[3] for entry in outputs], axis=0).astype(jnp.bfloat16)
    grad_down = jnp.stack([entry[4] for entry in outputs], axis=0).astype(jnp.bfloat16)
    slot_grid = slots.reshape(group_rows, top_count)

    def combine(table):
        picked = table.reshape(expert_total * slot_most, -1)[slot_grid]
        return jnp.sum(picked, axis=1)

    column_out, column_in = (
        lax.psum_scatter(
            out_rows.astype(jnp.float32).astype(jnp.bfloat16), "tp", scatter_dimension=2, tiled=True
        ).astype(jnp.float32),
        lax.psum_scatter(
            in_rows.astype(jnp.float32).astype(jnp.bfloat16), "tp", scatter_dimension=2, tiled=True
        ).astype(jnp.float32),
    )
    back_out, back_in = (
        lax.all_to_all(
            column_out.astype(jnp.bfloat16), ("dp", "ctx"), split_axis=0, concat_axis=0, tiled=True
        ).astype(column_out.dtype),
        lax.all_to_all(
            column_in.astype(jnp.bfloat16), ("dp", "ctx"), split_axis=0, concat_axis=0, tiled=True
        ).astype(column_in.dtype),
    )
    layer_out, grad_tokens = (
        lax.all_to_all(
            combine(back_out).astype(jnp.bfloat16), "tp", split_axis=0, concat_axis=1, tiled=True
        ).astype(jnp.float32),
        lax.all_to_all(
            combine(back_in).astype(jnp.bfloat16), "tp", split_axis=0, concat_axis=1, tiled=True
        ).astype(jnp.float32),
    )
    return (
        layer_out.astype(jnp.bfloat16),
        grad_tokens.astype(jnp.bfloat16),
        grad_gate,
        grad_up,
        grad_down,
    )


def select_rows(order, row_count):
    rows = lax.broadcasted_iota(jnp.int32, (row_count, order.shape[-1]), 0)
    return rows == order


class Place:
    def __init__(self):
        self.ring = lax.axis_size("dp")
        self.z, self.x = lax.axis_index("dp"), lax.axis_index("ctx")
        tp = lax.axis_index("tp")
        self.y, self.c = tp // 2, tp % 2

    def device(self, z=None, x=None, y=None, c=None):
        pick = lambda value, own: own if value is None else value
        tp = pick(y, self.y) * 2 + pick(c, self.c)
        return (pick(z, self.z), pick(x, self.x), tp)

    def meet(self):
        barrier = pltpu.get_barrier_semaphore()
        others = [self.core_peer(), self.x_peer(), self.y_peer()]
        others += [self.device(z=lax.rem(self.z + k, self.ring)) for k in range(1, self.ring)]
        for other in others:
            pl.semaphore_signal(
                barrier, inc=1, device_id=other, device_id_type=pl.DeviceIdType.MESH
            )
        pl.semaphore_wait(barrier, len(others))

    def core_peer(self):
        return self.device(c=1 - self.c)

    def x_peer(self):
        return self.device(x=1 - self.x)

    def y_peer(self):
        return self.device(y=1 - self.y)


def start_send(source, target, send_sem, recv_sem, device):
    copy = pltpu.make_async_remote_copy(
        src_ref=source,
        dst_ref=target,
        send_sem=send_sem,
        recv_sem=recv_sem,
        device_id=device,
        device_id_type=pl.DeviceIdType.MESH,
    )
    copy.start()
    return copy


def gather_kernel(own_a, own_b, all_a, all_b, send_sems, recv_sems, local_sems):
    at = Place()
    z, x, y, c, ring = at.z, at.x, at.y, at.c, at.ring
    own, full = (own_a, own_b), (all_a, all_b)
    stay = []
    for h in range(2):
        copy = pltpu.make_async_copy(own[h], full[h].at[z, x, y, c], local_sems.at[h])
        copy.start()
        stay.append(copy)
    at.meet()
    sems = lambda stage, h, k: (send_sems.at[stage, h, k], recv_sems.at[stage, h, k])
    first, second, third, along = {}, {}, {}, {}
    peers = ((at.x_peer(), at.y_peer()), (at.y_peer(), at.x_peer()))
    for h in range(2):
        here = full[h].at[z, x, y, c]
        first[h, 0] = start_send(own[h], here, *sems(1, h, 0), peers[h][0])
        for k in range(1, ring):
            away = at.device(z=lax.rem(z + k, ring))
            along[h, k] = start_send(own[h], here, *sems(0, h, k), away)
    for copy in stay:
        copy.wait()
    for step in range(ring + 2):
        for h in range(2):
            k = step
            if 0 < k < ring:
                along[h, k].wait_recv()
                block = full[h].at[lax.rem(z - k + ring, ring), x, y, c]
                first[h, k] = start_send(block, block, *sems(1, h, k), peers[h][0])
        for h in range(2):
            k = step - 1
            if 0 <= k < ring:
                zz = lax.rem(z - k + ring, ring)
                first[h, k].wait_recv()
                block = full[h].at[zz, :, y, c] if h == 0 else full[h].at[zz, x, :, c]
                second[h, k] = start_send(block, block, *sems(2, h, k), peers[h][1])
        for h in range(2):
            k = step - 2
            if 0 <= k < ring:
                second[h, k].wait_recv()
                block = full[h].at[lax.rem(z - k + ring, ring), :, :, c]
                third[h, k] = start_send(block, block, *sems(3, h, k), at.core_peer())
    for copy in third.values():
        copy.wait_recv()
    for copies in (along, first, second, third):
        for copy in copies.values():
            copy.wait_send()


def gather_all(own_a, own_b):
    ring = lax.axis_size("dp")
    full = lambda own: jax.ShapeDtypeStruct((ring, 2, 2, 2, *own.shape), own.dtype)
    anywhere = pl.BlockSpec(memory_space=pl.ANY)
    return pl.pallas_call(
        gather_kernel,
        in_specs=[anywhere, anywhere],
        out_specs=[anywhere, anywhere],
        out_shape=[full(own_a), full(own_b)],
        scratch_shapes=[
            pltpu.SemaphoreType.DMA((4, 2, ring)),
            pltpu.SemaphoreType.DMA((4, 2, ring)),
            pltpu.SemaphoreType.DMA((2,)),
        ],
        compiler_params=pltpu.CompilerParams(collective_id=0, has_side_effects=True),
        name="gather_all",
    )(own_a, own_b)


def reduce_kernel(sums, out_a, out_b, got1, sum1, got2, sum2, got3, sum3, got4, send_sems, recv_sems):
    at = Place()
    z, x, y, c, ring = at.z, at.x, at.y, at.c, at.ring
    f32, bf16 = jnp.float32, jnp.bfloat16
    at.meet()
    sems = lambda stage, h, k: (send_sems.at[stage, h, k], recv_sems.at[stage, h, k])
    peers = ((at.y_peer(), at.x_peer()), (at.x_peer(), at.y_peer()))
    copies = [{}, {}, {}, {}]
    pairs = [(k, h) for k in range(ring) for h in range(2)]
    aim = [lax.rem(z + 1 + k, ring) for k in range(ring)]
    for k, h in pairs:
        copies[0][h, k] = start_send(
            sums.at[h, aim[k], :, :, 1 - c], got1.at[h, k], *sems(0, h, k), at.core_peer()
        )

    def fold_core(h, k):
        copies[0][h, k].wait_recv()
        sum1[h, k] = (sums[h, aim[k], :, :, c].astype(f32) + got1[h, k].astype(f32)).astype(bf16)
        part = sum1.at[h, k, :, 1 - y] if h == 0 else sum1.at[h, k, 1 - x]
        copies[1][h, k] = start_send(part, got2.at[h, k], *sems(1, h, k), peers[h][0])

    def fold_first(h, k):
        copies[1][h, k].wait_recv()
        mine = sum1[h, k, :, y] if h == 0 else sum1[h, k, x]
        sum2[h, k] = (mine.astype(f32) + got2[h, k].astype(f32)).astype(bf16)
        part = sum2.at[h, k, 1 - x] if h == 0 else sum2.at[h, k, 1 - y]
        copies[2][h, k] = start_send(part, got3.at[h, k], *sems(2, h, k), peers[h][1])

    def fold_second(h, k):
        copies[2][h, k].wait_recv()
        mine = sum2[h, k, x] if h == 0 else sum2[h, k, y]
        sum3[h, k] = (mine.astype(f32) + got3[h, k].astype(f32)).astype(bf16)
        if k < ring - 1:
            copies[3][h, k] = start_send(
                sum3.at[h, k], got4.at[h, k], *sems(3, h, k), at.device(z=aim[k])
            )

    for step in range(ring + 2):
        for late, fold in enumerate((fold_core, fold_first, fold_second)):
            if 0 <= step - late < ring:
                for h in range(2):
                    fold(h, step - late)
    for h, out in enumerate((out_a, out_b)):
        total = sum3[h, ring - 1].astype(f32)
        for k in range(ring - 1):
            copies[3][h, k].wait_recv()
            total = total + got4[h, k].astype(f32)
        out[...] = total.astype(bf16)
    for stage in copies:
        for copy in stage.values():
            copy.wait_send()


def reduce_all(sums):
    _, ring, _, _, _, rows, width = sums.shape
    out = jax.ShapeDtypeStruct((rows, width), sums.dtype)
    in_vmem = pl.BlockSpec(memory_space=pltpu.VMEM)
    table = lambda *lead: pltpu.VMEM((2, ring, *lead, rows, width), sums.dtype)
    return pl.pallas_call(
        reduce_kernel,
        in_specs=[in_vmem],
        out_specs=[in_vmem, in_vmem],
        out_shape=[out, out],
        scratch_shapes=[
            table(2, 2), table(2, 2), table(2), table(2), table(), table(), table(),
            pltpu.SemaphoreType.DMA((4, 2, ring)),
            pltpu.SemaphoreType.DMA((4, 2, ring)),
        ],
        compiler_params=pltpu.CompilerParams(
            collective_id=1, has_side_effects=True, vmem_limit_bytes=60 << 20
        ),
        name="reduce_all",
    )(sums)


def rows_kernel(
    tokens, grads, order_row, scale_row, order_col, gate_w, up_w, down_w,
    inputs_out, cotangent_out, act_out, gate_pre_out, up_pre_out, sums_out,
    out_rows, in_rows, all_inputs, all_cotangents,
):
    f32, bf16 = jnp.float32, jnp.bfloat16
    expert = pl.program_id(0)
    expert_count = order_col.shape[1]
    row_count = inputs_out.shape[1]
    token_count, width = tokens.shape

    @pl.when(expert == 0)
    def _():
        pick = jnp.concatenate(
            [
                jnp.where(select_rows(order_row[e], row_count), 1.0, 0.0).astype(bf16)
                for e in range(expert_count)
            ],
            axis=0,
        )
        step = min(512, width)
        for left in range(0, width, step):
            for table, rows in ((tokens, all_inputs), (grads, all_cotangents)):
                rows[:, left : left + step] = jnp.dot(
                    pick, table[:, left : left + step], preferred_element_type=f32
                ).astype(bf16)

    here = pl.ds(pl.multiple_of(expert * row_count, row_count), row_count)
    picked = select_rows(order_row[expert], row_count)
    row_scale = jnp.sum(jnp.where(picked, scale_row[0], 0.0), axis=1, keepdims=True)
    inputs = all_inputs[here, :]
    cotangent = all_cotangents[here, :]
    inputs_out[0] = inputs
    cotangent_out[0] = cotangent
    gate = jnp.dot(inputs, gate_w[0], preferred_element_type=f32)
    upward = jnp.dot(inputs, up_w[0], preferred_element_type=f32)
    backward = lax.dot_general(cotangent, down_w[0], contract_last, preferred_element_type=f32)
    sigmoid_gate = jax.nn.sigmoid(gate)
    silu = row_scale * gate * sigmoid_gate
    act = (silu * upward).astype(bf16)
    gate_pre = (
        backward * row_scale * upward * sigmoid_gate * (1.0 + gate * (1.0 - sigmoid_gate))
    ).astype(bf16)
    up_pre = (backward * silu).astype(bf16)
    act_out[0] = act
    gate_pre_out[0] = gate_pre
    up_pre_out[0] = up_pre
    out_rows[here, :] = jnp.dot(act, down_w[0], preferred_element_type=f32).astype(bf16)
    in_rows[here, :] = (
        lax.dot_general(gate_pre, gate_w[0], contract_last, preferred_element_type=f32)
        + lax.dot_general(up_pre, up_w[0], contract_last, preferred_element_type=f32)
    ).astype(bf16)

    @pl.when(expert == expert_count - 1)
    def _():
        lanes = lax.broadcasted_iota(jnp.int32, (token_count, row_count), 1)
        place = jnp.concatenate(
            [
                jnp.where(lanes == order_col[:, e : e + 1], 1.0, 0.0).astype(bf16)
                for e in range(expert_count)
            ],
            axis=1,
        )
        sums_out[0] = jnp.dot(
            place, out_rows[...], preferred_element_type=f32
        ).astype(bf16)
        sums_out[1] = jnp.dot(
            place, in_rows[...], preferred_element_type=f32
        ).astype(bf16)


def weights_kernel(inputs, cotangent, act, gate_pre, up_pre, gate_out, up_out, down_out):
    f32, bf16 = jnp.float32, jnp.bfloat16
    gate_out[0] = lax.dot_general(
        inputs[0], gate_pre[0], contract_first, preferred_element_type=f32
    ).astype(bf16)
    up_out[0] = lax.dot_general(
        inputs[0], up_pre[0], contract_first, preferred_element_type=f32
    ).astype(bf16)
    down_out[0] = lax.dot_general(
        act[0], cotangent[0], contract_first, preferred_element_type=f32
    ).astype(bf16)


def gathered_shards(tokens, grad_out, expert_ids, router_weights, w_gate, w_up, w_down):
    f32, bf16, i32 = jnp.float32, jnp.bfloat16, jnp.int32
    own_tokens, width = tokens.shape
    group_rows, top_count = expert_ids.shape
    experts, _, hidden = w_gate.shape
    groups = lax.axis_size(("dp", "ctx"))
    row_count = groups * (2 * group_rows * top_count // (groups * experts))
    start = lax.axis_index("tp") * own_tokens
    own_ids = lax.dynamic_slice_in_dim(expert_ids, start, own_tokens, 0)
    own_weights = lax.dynamic_slice_in_dim(router_weights, start, own_tokens, 0)
    routing = jnp.concatenate(
        [own_ids.astype(bf16), own_weights, jnp.zeros((own_tokens, 128 - 2 * top_count), bf16)],
        axis=1,
    )
    all_tokens, carried = gather_all(tokens, jnp.concatenate([grad_out, routing], axis=1))
    all_tokens, carried = all_tokens.reshape(-1, width), carried.reshape(-1, width + 128)
    total = carried.shape[0]
    ids = carried[:, width : width + top_count].astype(i32)
    weights = carried[:, width + top_count : width + 2 * top_count].astype(f32)
    first = lax.axis_index(("dp", "ctx")) * experts
    named = ids[:, None, :] == (first + jnp.arange(experts, dtype=i32))[None, :, None]
    scale = jnp.sum(jnp.where(named, weights[:, None, :], 0.0), axis=2)
    hit = jnp.any(named, axis=2)
    place = jnp.arange(total, dtype=i32)
    earlier = (place[:, None] > place[None, :]).astype(bf16)
    rank = jnp.dot(earlier, hit.astype(bf16), preferred_element_type=f32).astype(i32)
    order_col = jnp.where(hit, rank, -1)
    order_row = order_col.T.reshape(experts, 1, total)
    scale_row = scale.T.reshape(experts, 1, total)

    whole = lambda *shape: pl.BlockSpec(shape, lambda e: (0,) * len(shape))
    each = lambda *shape: pl.BlockSpec((1, *shape), lambda e: (e, 0, 0))
    rows_shape = lambda n: jax.ShapeDtypeStruct((experts, row_count, n), bf16)
    matmul = 2 * experts * row_count * width * hidden
    inputs, cotangent, act, gate_pre, up_pre, sums = pl.pallas_call(
        rows_kernel,
        grid=(experts,),
        in_specs=[
            whole(total, width),
            whole(total, width),
            whole(experts, 1, total),
            each(1, total),
            whole(total, experts),
            each(width, hidden),
            each(width, hidden),
            each(hidden, width),
        ],
        out_specs=[
            each(row_count, width),
            each(row_count, width),
            each(row_count, hidden),
            each(row_count, hidden),
            each(row_count, hidden),
            whole(2, total, width),
        ],
        out_shape=[
            rows_shape(width),
            rows_shape(width),
            rows_shape(hidden),
            rows_shape(hidden),
            rows_shape(hidden),
            jax.ShapeDtypeStruct((2, total, width), bf16),
        ],
        scratch_shapes=[
            pltpu.VMEM((experts * row_count, width), bf16),
            pltpu.VMEM((experts * row_count, width), bf16),
            pltpu.VMEM((experts * row_count, width), bf16),
            pltpu.VMEM((experts * row_count, width), bf16),
        ],
        compiler_params=pltpu.CompilerParams(vmem_limit_bytes=60 << 20),
        cost_estimate=pl.CostEstimate(
            flops=6 * matmul, bytes_accessed=6 * experts * width * hidden, transcendentals=0
        ),
        name="expert_rows",
    )(all_tokens, carried, order_row, scale_row, order_col, w_gate, w_up, w_down)
    layer_out, grad_tokens = reduce_all(
        sums.reshape(2, lax.axis_size("dp"), 2, 2, 2, own_tokens, width)
    )
    grad_gate, grad_up, grad_down = pl.pallas_call(
        weights_kernel,
        grid=(experts,),
        in_specs=[
            each(row_count, width),
            each(row_count, width),
            each(row_count, hidden),
            each(row_count, hidden),
            each(row_count, hidden),
        ],
        out_specs=[each(width, hidden), each(width, hidden), each(hidden, width)],
        out_shape=[
            jax.ShapeDtypeStruct(w_gate.shape, bf16),
            jax.ShapeDtypeStruct(w_up.shape, bf16),
            jax.ShapeDtypeStruct(w_down.shape, bf16),
        ],
        compiler_params=pltpu.CompilerParams(vmem_limit_bytes=60 << 20),
        cost_estimate=pl.CostEstimate(
            flops=3 * matmul, bytes_accessed=6 * experts * width * hidden, transcendentals=0
        ),
        name="expert_weights",
    )(inputs, cotangent, act, gate_pre, up_pre)
    return layer_out, grad_tokens, grad_gate, grad_up, grad_down


def solution(mesh):
    def per_device(tokens, *rest):
        devices = lax.axis_size(("dp", "ctx", "tp"))
        few = tokens.shape[0] * devices <= 1024
        few = few and lax.axis_size("ctx") == 2 and lax.axis_size("tp") == 4
        return (gathered_shards if few else shards)(tokens, *rest)

    placed = (
        P(("dp", "ctx", "tp"), None),
        P(("dp", "ctx", "tp"), None),
        P(("dp", "ctx"), None),
        P(("dp", "ctx"), None),
        P(("dp", "ctx"), None, "tp"),
        P(("dp", "ctx"), None, "tp"),
        P(("dp", "ctx"), "tp", None),
    )
    return jax.shard_map(
        per_device,
        mesh=mesh,
        in_specs=placed,
        out_specs=(
            P(("dp", "ctx", "tp"), None),
            P(("dp", "ctx", "tp"), None),
            P(("dp", "ctx"), None, "tp"),
            P(("dp", "ctx"), None, "tp"),
            P(("dp", "ctx"), "tp", None),
        ),
        check_vma=False,
    )
```
